1024 devices in a mesh: expert: 16 (over x, z_lo), block: 64 (over z_hi, y, core).
Axes of the slice: x: 8, y: 8, z: 8 (z_hi: 4, z_lo: 2; z = z_hi * 2 + z_lo), core: 2. Of those that a mesh axis runs over, the one named last changes fastest.
Arguments:
- iterate: bfloat16 [16, 7168, 2048], P(None, ('expert', 'block')), may hold values from -0.046875 to 0.046875
Outputs:
- update: bfloat16 [16, 64, 448, 512], P('expert', 'block')
The draws below stay inside these ranges and needn't reach their ends.
All inputs are finite; a program needn't handle non-finite values.
Results may differ from the reference program's by a relative error of at most 0.015.
Values may be sent and summed in bfloat16 or wider, within the bound.
No kernel may reach another device: no remote copies, remote signals or barrier semaphores. Data moves between devices by JAX's collectives and lax.ppermute only.
A program may use at most 32 MiB of HBM per device.

```python
import math
import jax
import jax.numpy as jnp
from jax import lax

D = 7168
MOE_FF = 2048
EXPERTS = 16
GROUP_ROWS = 448
N_EXPERT = 16
N_BLOCK = 64


def block_scale(stream_key, extent, split, low, largest):
    def one(axis_at, parts):
        heights = jax.random.uniform(jax.random.fold_in(jax.random.fold_in(stream_key, 6), axis_at), (parts,), jnp.float32, low / len(split), largest / len(split))
        return jnp.repeat(jnp.exp(heights), extent[axis_at] // parts).reshape((-1,) + (1,) * (len(extent) - axis_at - 1))

    level = one(*split[0])
    for cut in split[1:]:
        level = level * one(*cut)
    return level


def gaussian(stream_key, extent, scale, limit, shards=(), held_as=jnp.bfloat16):
    array = scale * jax.random.normal(stream_key, extent, jnp.float32)
    if shards:
        array = array * block_scale(stream_key, extent, shards, -0.22, 0.18)
    return jnp.clip(array, -limit, limit).astype(held_as)


def setup_inputs(seed: int = 0) -> dict:
    key_of = jax.random.split(jax.random.key(seed), 2)
    return {
        "iterate": gaussian(key_of[0], (EXPERTS, D, MOE_FF), (1.0 / (D ** 0.5 + MOE_FF ** 0.5)), 0.046875, ((1, 1024),)),
    }


def one_expert(matrix):
    rows_each = D // (N_EXPERT * N_BLOCK)
    grid_rows = N_BLOCK // 4
    blocked = matrix.reshape(N_EXPERT, grid_rows, 4, rows_each, MOE_FF)
    blocked = jnp.transpose(blocked, (1, 2, 0, 3, 4)).reshape(grid_rows, GROUP_ROWS, MOE_FF)

    def add_partial(total, piece):
        partial_value = jnp.dot(piece.T, piece, preferred_element_type=jnp.float32).astype(jnp.bfloat16)
        partial_value = lax.optimization_barrier(partial_value)
        return (total + partial_value.astype(jnp.float32), None)
    summed, unused = lax.scan(add_partial, jnp.zeros((MOE_FF, MOE_FF), jnp.float32), blocked)
    gram = summed.astype(jnp.bfloat16)
    flat = blocked.reshape(grid_rows * GROUP_ROWS, MOE_FF)
    first = jnp.dot(flat, gram, preferred_element_type=jnp.float32).astype(jnp.bfloat16)
    second = jnp.dot(first, gram, preferred_element_type=jnp.float32)
    scale = 0.2 * math.sqrt(max(D, MOE_FF))
    fresh = scale * (3.4445 * flat.astype(jnp.float32) - 4.775 * first.astype(jnp.float32) + 2.0315 * second)
    fresh = fresh.reshape(grid_rows, GROUP_ROWS, 4, MOE_FF // 4)
    fresh = jnp.transpose(fresh, (0, 2, 1, 3)).reshape(N_BLOCK, GROUP_ROWS, MOE_FF // 4)
    return fresh.astype(jnp.bfloat16)

def reference(iterate):
    return lax.map(one_expert, iterate)
```

```python
import functools
import math

import jax
import jax.numpy as jnp
from jax import lax
from jax.experimental import pallas as pl
from jax.experimental.pallas import tpu as pltpu
from jax.sharding import PartitionSpec as P

D = 7168
MOE_FF = 2048
N_Y = 8
N_Z = 4
SIDE = 128
STRIP = 9 * SIDE
PAIR = 10 * SIDE
WIDE = MOE_FF + PAIR
SCALE = 0.2 * math.sqrt(max(D, MOE_FF))
BF = jnp.bfloat16
F32 = jnp.float32


def block_pairs(shift_y, shift_z, flip):
    pairs = []
    for z in range(N_Z):
        for y in range(N_Y):
            for c in range(2):
                target = ((z + shift_z) % N_Z * N_Y + (y + shift_y) % N_Y) * 2 + (c ^ flip)
                pairs.append(((z * N_Y + y) * 2 + c, target))
    return pairs


def send(value, shift_y=0, shift_z=0, flip=0):
    return lax.ppermute(value, "block", block_pairs(shift_y, shift_z, flip))


def z_groups():
    return [[z * 16 + j for z in range(N_Z)] for j in range(16)]


def row_groups():
    return [[4 * p + q for q in range(4)] for p in range(16)]


def apply_kernel(where_ref, x_ref, *refs):
    mine, other = refs[:9], refs[9:18]
    out_ref, wide, acc, direct, turned = refs[18:]
    y, core = where_ref[0], where_ref[1]
    rows = x_ref.shape[0]

    def place(pieces, half):
        top = pl.multiple_of(half * SIDE, SIDE)
        for r in range(8):
            i = lax.rem(y + r, 8)
            if r < 4:
                parts = [(0, SIDE, pieces[r])]
            elif r == 4:
                parts = [(0, SIDE // 2, pieces[4]), (SIDE // 2, SIDE // 2, pieces[5])]
            else:
                parts = [(0, SIDE, pieces[r + 1])]
            for first, count, ref in parts:
                at = pl.ds(pl.multiple_of(top + first, 16), count)
                direct[i, at, pl.ds(top, STRIP)] = ref[...]
                turned[i, at, pl.ds(top, 7 * SIDE)] = ref[:, SIDE : 8 * SIDE]

    zero = jnp.zeros((SIDE, SIDE), BF)
    for i in range(8):
        direct[i, 0:SIDE, STRIP:PAIR] = zero
        direct[i, SIDE : 2 * SIDE, 0:SIDE] = zero
        turned[i, 0:SIDE, 7 * SIDE : 8 * SIDE] = zero
        turned[i, SIDE : 2 * SIDE, 0:SIDE] = zero
    place(mine, core)
    place(other, 1 - core)

    def times_gram(value):
        wide[:, 0:MOE_FF] = value
        wide[:, MOE_FF:WIDE] = value[:, 0:PAIR]
        acc[...] = jnp.zeros_like(acc)

        def step(i, carry):
            start = pl.multiple_of(i * 2 * SIDE, 2 * SIDE)
            acc[:, pl.ds(start, PAIR)] += lax.dot_general(
                wide[:, pl.ds(start, 2 * SIDE)], direct[i],
                (((1,), (0,)), ((), ())), preferred_element_type=F32,
            )
            acc[:, pl.ds(start, 2 * SIDE)] += lax.dot_general(
                wide[:, pl.ds(pl.multiple_of(start + SIDE, SIDE), 8 * SIDE)], turned[i],
                (((1,), (1,)), ((), ())), preferred_element_type=F32,
            )
            return carry

        lax.fori_loop(0, 8, step, 0)
        return jnp.concatenate(
            [acc[:, 0:PAIR] + acc[:, MOE_FF:WIDE], acc[:, PAIR:MOE_FF]], axis=1
        )

    x = x_ref[...]
    first = times_gram(x).astype(BF)
    second = times_gram(first)
    fresh = SCALE * (3.4445 * x.astype(F32) - 4.775 * first.astype(F32) + 2.0315 * second)
    fresh = fresh.astype(BF)
    for q in range(4):
        out_ref[q] = fresh[:, q * 512 : (q + 1) * 512]


def apply_gram(where, x, mine, other):
    rows = x.shape[0]
    vmem = pl.BlockSpec(memory_space=pltpu.VMEM)
    return pl.pallas_call(
        apply_kernel,
        out_shape=jax.ShapeDtypeStruct((4, rows, 512), BF),
        in_specs=[pl.BlockSpec(memory_space=pltpu.SMEM)] + [vmem] * 19,
        out_specs=vmem,
        scratch_shapes=[
            pltpu.VMEM((rows, WIDE), BF),
            pltpu.VMEM((rows, WIDE), F32),
            pltpu.VMEM((8, 2 * SIDE, PAIR), BF),
            pltpu.VMEM((8, 2 * SIDE, 8 * SIDE), BF),
        ],
        compiler_params=pltpu.CompilerParams(vmem_limit_bytes=40 * 2**20),
        cost_estimate=pl.CostEstimate(
            flops=4 * rows * MOE_FF * MOE_FF, bytes_accessed=5 * 2**20, transcendentals=0
        ),
    )(where, x, *mine, *other)


def shards(iterate):
    index = lax.axis_index("block")
    core = index % 2
    y = index // 2 % N_Y
    own = lax.all_to_all(iterate, "expert", split_axis=0, concat_axis=1, tiled=True)[0]
    both = jnp.concatenate([own, send(own, flip=1)], 0)
    ring = jnp.concatenate([both, both[:, : 8 * SIDE]], 1)

    def partial(d):
        at = (2 * ((y + d) % N_Y) + core) * SIDE
        left = lax.dynamic_slice_in_dim(ring, at, SIDE, 1)
        right = lax.dynamic_slice_in_dim(ring, at, STRIP, 1)
        return lax.dot_general(left, right, (((0,), (0,)), ((), ())), preferred_element_type=F32)

    half = SIDE // 2
    far = partial(4).astype(BF)
    up, down = far[:half], far[half:]
    for d in (3, 2, 1, 0):
        up, down = send(up, shift_y=1), send(down, shift_y=-1)
        if d == 3:
            a, b = partial(3), partial(-3)
            up = jnp.concatenate([a[:half] + up.astype(F32), a[half:]], 0).astype(BF)
            down = jnp.concatenate([b[:half], b[half:] + down.astype(F32)], 0).astype(BF)
        elif d:
            up = (partial(d) + up.astype(F32)).astype(BF)
            down = (partial(-d) + down.astype(F32)).astype(BF)
    summed = (partial(0) + up.astype(F32) + down.astype(F32)).astype(BF)
    parts = lax.all_to_all(summed, "block", 0, 0, axis_index_groups=z_groups(), tiled=True)
    parts = parts.reshape(N_Z, SIDE // N_Z, STRIP).astype(F32)
    piece = parts.sum(0).astype(BF)
    strip = lax.all_gather(piece, "block", axis=0, axis_index_groups=z_groups(), tiled=True)
    ups, downs = [strip], [strip]
    for d in range(1, 5):
        a, b = ups[-1], downs[-1]
        if d == 4:
            a, b = a[:half], b[half:]
        ups.append(send(a, shift_y=1))
        downs.append(send(b, shift_y=-1))
    mine = downs[:4] + [ups[4], downs[4], ups[3], ups[2], ups[1]]
    near = send(jnp.stack([strip, downs[1], downs[2], ups[2], ups[1]]), flip=1)
    far = send(jnp.concatenate([downs[3], ups[4], downs[4], ups[3]], 0), flip=1)
    other = [near[0], near[1], near[2], far[:SIDE], far[SIDE : SIDE + half], far[SIDE + half : 2 * SIDE], far[2 * SIDE :], near[3], near[4]]
    where = jnp.stack([y, core]).astype(jnp.int32)
    fresh = apply_gram(where, own, mine, other)
    out = lax.all_to_all(fresh, "block", 0, 1, axis_index_groups=row_groups(), tiled=True)
    return out[:, None]


def solution(mesh):
    return jax.shard_map(
        shards,
        mesh=mesh,
        in_specs=(P(None, ("expert", "block"), None),),
        out_specs=P("expert", "block", None, None),
        check_vma=False,
    )
```

```python
import math

import jax
import jax.numpy as jnp
from jax import lax
from jax.experimental import pallas as pl
from jax.experimental.pallas import tpu as pltpu
from jax.sharding import PartitionSpec as P

D = 7168
MOE_FF = 2048
N_Y = 8
N_Z = 4
SIDE = 128
SLAB = SIDE // N_Z
STRIP = 9 * SIDE
PAIR = 10 * SIDE
WIDE = MOE_FF + PAIR
SCALE = 0.2 * math.sqrt(max(D, MOE_FF))
BF = jnp.bfloat16
F32 = jnp.float32


def swap_cores(value):
    return lax.ppermute(value, "block", [(i, i ^ 1) for i in range(2 * N_Y * N_Z)])


def core_groups():
    return [[2 * i + c for i in range(N_Y * N_Z)] for c in range(2)]


def row_groups():
    return [[4 * p + q for q in range(4)] for p in range(16)]


def strips_kernel(core_ref, own_ref, other_ref, out_ref, wide):
    rows = own_ref.shape[0]
    for first, ref in ((0, own_ref), (rows, other_ref)):
        wide[first : first + rows, 0:MOE_FF] = ref[...]
        wide[first : first + rows, MOE_FF : MOE_FF + 8 * SIDE] = ref[:, 0 : 8 * SIDE]

    def strip(y, carry):
        start = pl.multiple_of((2 * y + core_ref[0]) * SIDE, SIDE)
        value = lax.dot_general(
            wide[:, pl.ds(start, SIDE)], wide[:, pl.ds(start, STRIP)],
            (((0,), (0,)), ((), ())), preferred_element_type=F32,
        ).astype(BF)
        for z in range(N_Z):
            out_ref[z, y] = value[z * SLAB : (z + 1) * SLAB]
        return carry

    lax.fori_loop(0, N_Y, strip, 0)


def make_strips(core, own, other):
    vmem = pl.BlockSpec(memory_space=pltpu.VMEM)
    rows = own.shape[0]
    return pl.pallas_call(
        strips_kernel,
        out_shape=jax.ShapeDtypeStruct((N_Z, N_Y, SLAB, STRIP), BF),
        in_specs=[pl.BlockSpec(memory_space=pltpu.SMEM), vmem, vmem],
        out_specs=vmem,
        scratch_shapes=[pltpu.VMEM((2 * rows, MOE_FF + 8 * SIDE), BF)],
        compiler_params=pltpu.CompilerParams(vmem_limit_bytes=32 * 2**20),
        cost_estimate=pl.CostEstimate(
            flops=4 * rows * SIDE * STRIP * N_Y, bytes_accessed=4 * 2**20, transcendentals=0
        ),
    )(core, own, other)


def apply_kernel(core_ref, x_ref, mine_ref, other_ref, out_ref, wide, acc, direct, turned):
    zero = jnp.zeros((SIDE, SIDE), BF)
    for ref, half in ((mine_ref, core_ref[0]), (other_ref, 1 - core_ref[0])):
        top = pl.multiple_of(half * SIDE, SIDE)
        for y in range(N_Y):
            for z in range(N_Z):
                at = pl.ds(pl.multiple_of(top + z * SLAB, SLAB), SLAB)
                direct[y, at, pl.ds(top, STRIP)] = ref[z, y]
                turned[y, at, pl.ds(top, 7 * SIDE)] = ref[z, y, :, SIDE : 8 * SIDE]
    for i in range(N_Y):
        direct[i, 0:SIDE, STRIP:PAIR] = zero
        direct[i, SIDE : 2 * SIDE, 0:SIDE] = zero
        turned[i, 0:SIDE, 7 * SIDE : 8 * SIDE] = zero
        turned[i, SIDE : 2 * SIDE, 0:SIDE] = zero

    def times_gram(value):
        wide[:, 0:MOE_FF] = value
        wide[:, MOE_FF:WIDE] = value[:, 0:PAIR]
        acc[...] = jnp.zeros_like(acc)

        def step(i, carry):
            start = pl.multiple_of(i * 2 * SIDE, 2 * SIDE)
            acc[:, pl.ds(start, PAIR)] += lax.dot_general(
                wide[:, pl.ds(start, 2 * SIDE)], direct[i],
                (((1,), (0,)), ((), ())), preferred_element_type=F32,
            )
            acc[:, pl.ds(start, 2 * SIDE)] += lax.dot_general(
                wide[:, pl.ds(pl.multiple_of(start + SIDE, SIDE), 8 * SIDE)], turned[i],
                (((1,), (1,)), ((), ())), preferred_element_type=F32,
            )
            return carry

        lax.fori_loop(0, N_Y, step, 0)
        return jnp.concatenate(
            [acc[:, 0:PAIR] + acc[:, MOE_FF:WIDE], acc[:, PAIR:MOE_FF]], axis=1
        )

    x = x_ref[...]
    first = times_gram(x).astype(BF)
    second = times_gram(first)
    fresh = SCALE * (3.4445 * x.astype(F32) - 4.775 * first.astype(F32) + 2.0315 * second)
    fresh = fresh.astype(BF)
    for q in range(4):
        out_ref[q] = fresh[:, q * 512 : (q + 1) * 512]


def apply_gram(core, x, mine, other):
    rows = x.shape[0]
    vmem = pl.BlockSpec(memory_space=pltpu.VMEM)
    return pl.pallas_call(
        apply_kernel,
        out_shape=jax.ShapeDtypeStruct((4, rows, 512), BF),
        in_specs=[pl.BlockSpec(memory_space=pltpu.SMEM)] + [vmem] * 3,
        out_specs=vmem,
        scratch_shapes=[
            pltpu.VMEM((rows, WIDE), BF),
            pltpu.VMEM((rows, WIDE), F32),
            pltpu.VMEM((N_Y, 2 * SIDE, PAIR), BF),
            pltpu.VMEM((N_Y, 2 * SIDE, 8 * SIDE), BF),
        ],
        compiler_params=pltpu.CompilerParams(vmem_limit_bytes=40 * 2**20),
        cost_estimate=pl.CostEstimate(
            flops=4 * rows * MOE_FF * MOE_FF, bytes_accessed=5 * 2**20, transcendentals=0
        ),
    )(core, x, mine, other)


def shards(iterate):
    index = lax.axis_index("block")
    core = (index % 2).astype(jnp.int32)[None]
    own = lax.all_to_all(iterate, "expert", split_axis=0, concat_axis=1, tiled=True)[0]
    strips = make_strips(core, own, swap_cores(own))
    groups = core_groups()
    count = N_Y * N_Z
    strips = strips.reshape(count, SLAB, STRIP)
    parts = lax.all_to_all(strips, "block", 0, 0, axis_index_groups=groups, tiled=True)
    piece = parts.astype(F32).sum(0).astype(BF)
    copies = jnp.broadcast_to(piece[None], (count, SLAB, STRIP))
    mine = lax.all_to_all(copies, "block", 0, 0, axis_index_groups=groups, tiled=True)
    mine = mine.reshape(N_Z, N_Y, SLAB, STRIP)
    fresh = apply_gram(core, own, mine, swap_cores(mine))
    out = lax.all_to_all(fresh, "block", 0, 1, axis_index_groups=row_groups(), tiled=True)
    return out[:, None]


def solution(mesh):
    return jax.shard_map(
        shards,
        mesh=mesh,
        in_specs=(P(None, ("expert", "block"), None),),
        out_specs=P("expert", "block", None, None),
        check_vma=False,
    )
```

```python
import math

import jax
import jax.numpy as jnp
from jax import lax
from jax.experimental import pallas as pl
from jax.experimental.pallas import tpu as pltpu
from jax.sharding import Mesh
from jax.sharding import PartitionSpec as P

D = 7168
MOE_FF = 2048
N_Y = 8
N_Z = 4
SIDE = 128
SLAB = SIDE // N_Z
STRIP = 9 * SIDE
PAIR = 10 * SIDE
WIDE = MOE_FF + PAIR
SCALE = 0.2 * math.sqrt(max(D, MOE_FF))
BF = jnp.bfloat16
F32 = jnp.float32


def swap_cores(value):
    return lax.ppermute(value, "c", [(0, 1), (1, 0)])


def send_y(value, shift):
    return lax.ppermute(value, ("yh", "yl"), [(y, (y + shift) % N_Y) for y in range(N_Y)])


def strips_kernel(first_ref, *refs):
    out_ref, wide = refs[-2:]
    at = 0
    for ref in refs[:-2]:
        rows = ref.shape[0]
        wide[at : at + rows, 0:MOE_FF] = ref[...]
        wide[at : at + rows, MOE_FF : MOE_FF + 8 * SIDE] = ref[:, 0 : 8 * SIDE]
        at += rows

    def strip(y, carry):
        start = pl.multiple_of((4 * y + first_ref[0]) * SIDE, SIDE)
        value = lax.dot_general(
            wide[:, pl.ds(start, SIDE)], wide[:, pl.ds(start, STRIP)],
            (((0,), (0,)), ((), ())), preferred_element_type=F32,
        ).astype(BF)
        for z in range(N_Z):
            out_ref[z, y] = value[z * SLAB : (z + 1) * SLAB]
        return carry

    lax.fori_loop(0, N_Y // 2, strip, 0)


def make_strips(first, pieces):
    vmem = pl.BlockSpec(memory_space=pltpu.VMEM)
    rows = sum(piece.shape[0] for piece in pieces)
    return pl.pallas_call(
        strips_kernel,
        out_shape=jax.ShapeDtypeStruct((N_Z, N_Y // 2, SLAB, STRIP), BF),
        in_specs=[pl.BlockSpec(memory_space=pltpu.SMEM)] + [vmem] * len(pieces),
        out_specs=vmem,
        scratch_shapes=[pltpu.VMEM((rows, MOE_FF + 8 * SIDE), BF)],
        compiler_params=pltpu.CompilerParams(vmem_limit_bytes=32 * 2**20),
        cost_estimate=pl.CostEstimate(
            flops=rows * SIDE * STRIP * N_Y, bytes_accessed=4 * 2**20, transcendentals=0
        ),
    )(first, *pieces)


def apply_kernel(core_ref, x_ref, mine_ref, other_ref, out_ref, wide, acc, direct, turned):
    zero = jnp.zeros((SIDE, SIDE), BF)
    for ref, half in ((mine_ref, core_ref[0]), (other_ref, 1 - core_ref[0])):
        top = pl.multiple_of(half * SIDE, SIDE)
        for y in range(N_Y):
            for z in range(N_Z):
                at = pl.ds(pl.multiple_of(top + z * SLAB, SLAB), SLAB)
                direct[y, at, pl.ds(top, STRIP)] = ref[z, y]
                turned[y, at, pl.ds(top, 7 * SIDE)] = ref[z, y, :, SIDE : 8 * SIDE]
    for i in range(N_Y):
        direct[i, 0:SIDE, STRIP:PAIR] = zero
        direct[i, SIDE : 2 * SIDE, 0:SIDE] = zero
        turned[i, 0:SIDE, 7 * SIDE : 8 * SIDE] = zero
        turned[i, SIDE : 2 * SIDE, 0:SIDE] = zero

    def times_gram(value):
        wide[:, 0:MOE_FF] = value
        wide[:, MOE_FF:WIDE] = value[:, 0:PAIR]
        acc[...] = jnp.zeros_like(acc)

        def step(i, carry):
            start = pl.multiple_of(i * 2 * SIDE, 2 * SIDE)
            acc[:, pl.ds(start, PAIR)] += lax.dot_general(
                wide[:, pl.ds(start, 2 * SIDE)], direct[i],
                (((1,), (0,)), ((), ())), preferred_element_type=F32,
            )
            acc[:, pl.ds(start, 2 * SIDE)] += lax.dot_general(
                wide[:, pl.ds(pl.multiple_of(start + SIDE, SIDE), 8 * SIDE)], turned[i],
                (((1,), (1,)), ((), ())), preferred_element_type=F32,
            )
            return carry

        lax.fori_loop(0, N_Y, step, 0)
        return jnp.concatenate(
            [acc[:, 0:PAIR] + acc[:, MOE_FF:WIDE], acc[:, PAIR:MOE_FF]], axis=1
        )

    x = x_ref[...]
    first = times_gram(x).astype(BF)
    second = times_gram(first)
    fresh = SCALE * (3.4445 * x.astype(F32) - 4.775 * first.astype(F32) + 2.0315 * second)
    fresh = fresh.astype(BF)
    for q in range(4):
        out_ref[q] = fresh[:, q * 512 : (q + 1) * 512]


def apply_gram(core, x, mine, other):
    rows = x.shape[0]
    vmem = pl.BlockSpec(memory_space=pltpu.VMEM)
    return pl.pallas_call(
        apply_kernel,
        out_shape=jax.ShapeDtypeStruct((4, rows, 512), BF),
        in_specs=[pl.BlockSpec(memory_space=pltpu.SMEM)] + [vmem] * 3,
        out_specs=vmem,
        scratch_shapes=[
            pltpu.VMEM((rows, WIDE), BF),
            pltpu.VMEM((rows, WIDE), F32),
            pltpu.VMEM((N_Y, 2 * SIDE, PAIR), BF),
            pltpu.VMEM((N_Y, 2 * SIDE, 8 * SIDE), BF),
        ],
        compiler_params=pltpu.CompilerParams(vmem_limit_bytes=40 * 2**20),
        cost_estimate=pl.CostEstimate(
            flops=4 * rows * MOE_FF * MOE_FF, bytes_accessed=5 * 2**20, transcendentals=0
        ),
    )(core, x, mine, other)


def shards(iterate):
    core = lax.axis_index("c").astype(jnp.int32)
    parity = lax.axis_index("yl").astype(jnp.int32)
    own = lax.all_to_all(iterate, ("x", "zl"), split_axis=0, concat_axis=1, tiled=True)[0]
    half = own.shape[0] // 2
    near = jnp.concatenate([send_y(own[:half], 1), send_y(own[half:], -1)], 0)
    pieces = [own, swap_cores(own), near, swap_cores(near)]
    strips = make_strips((2 * parity + core)[None], pieces)
    strips = strips.reshape(N_Z * N_Y // 2, SLAB, STRIP)
    parts = lax.all_to_all(strips, ("zh", "yh"), 0, 0, tiled=True)
    piece = parts.astype(F32).sum(0).astype(BF)
    copies = jnp.broadcast_to(piece[None], (N_Z * N_Y, SLAB, STRIP))
    mine = lax.all_to_all(copies, ("zh", "yh", "yl"), 0, 0, tiled=True)
    mine = mine.reshape(N_Z, N_Y, SLAB, STRIP)
    fresh = apply_gram(core[None], own, mine, swap_cores(mine))
    out = lax.all_to_all(fresh, ("yl", "c"), 0, 1, tiled=True)
    return out[:, None]


def solution(mesh):
    names = ("x", "zl", "zh", "yh", "yl", "c")
    split = Mesh(mesh.devices.reshape(8, 2, N_Z, N_Y // 2, 2, 2), names)
    return jax.shard_map(
        shards,
        mesh=split,
        in_specs=(P(None, names, None),),
        out_specs=P(names[:2], names[2:], None, None),
        check_vma=False,
    )
```

```python
import functools
import math

import jax
import jax.numpy as jnp
from jax import lax
from jax.experimental import pallas as pl
from jax.experimental.pallas import tpu as pltpu
from jax.sharding import Mesh
from jax.sharding import PartitionSpec as P

D = 7168
MOE_FF = 2048
N_Y = 8
N_Z = 4
SIDE = 128
SLAB = SIDE // N_Z
STRIP = 8 * SIDE
PAIR = 10 * SIDE
TURN = 9 * SIDE
EXTRA = SIDE // 2 // N_Z
PIECE = 8 * SLAB + EXTRA
WIDE = MOE_FF + PAIR
SCALE = 0.2 * math.sqrt(max(D, MOE_FF))
BF = jnp.bfloat16
F32 = jnp.float32


def swap_cores(value):
    return lax.ppermute(value, "c", [(0, 1), (1, 0)])


def strips_kernel(core_ref, own_ref, other_ref, out_ref, wide):
    rows = own_ref.shape[0]
    for first, ref in ((0, own_ref), (rows, other_ref)):
        wide[first : first + rows, 0:MOE_FF] = ref[...]
        wide[first : first + rows, MOE_FF : MOE_FF + 8 * SIDE] = ref[:, 0 : 8 * SIDE]

    def times(left, right, width):
        return lax.dot_general(
            wide[:, pl.ds(pl.multiple_of(left, SIDE), SIDE)],
            wide[:, pl.ds(pl.multiple_of(right, SIDE), width)],
            (((0,), (0,)), ((), ())), preferred_element_type=F32,
        )

    def strip(y, carry):
        start = (2 * y + core_ref[0]) * SIDE
        value = times(start, start, STRIP).astype(BF)
        low = (2 * lax.rem(y, 4) + core_ref[0]) * SIDE
        extra = times(low, low + 8 * SIDE, SIDE)
        extra = jnp.where(y < 4, extra[: SIDE // 2], extra[SIDE // 2 :]).astype(BF)
        for z in range(N_Z):
            for m in range(8):
                out_ref[z, y, m * SLAB : (m + 1) * SLAB] = value[
                    z * SLAB : (z + 1) * SLAB, m * SIDE : (m + 1) * SIDE
                ]
            out_ref[z, y, 8 * SLAB : PIECE] = extra[z * EXTRA : (z + 1) * EXTRA]
        return carry

    lax.fori_loop(0, N_Y, strip, 0)


def make_strips(core, own, other):
    vmem = pl.BlockSpec(memory_space=pltpu.VMEM)
    rows = own.shape[0]
    return pl.pallas_call(
        strips_kernel,
        out_shape=jax.ShapeDtypeStruct((N_Z, N_Y, PIECE, SIDE), BF),
        in_specs=[pl.BlockSpec(memory_space=pltpu.SMEM), vmem, vmem],
        out_specs=vmem,
        scratch_shapes=[pltpu.VMEM((2 * rows, MOE_FF + 8 * SIDE), BF)],
        compiler_params=pltpu.CompilerParams(vmem_limit_bytes=32 * 2**20),
        cost_estimate=pl.CostEstimate(
            flops=4 * rows * SIDE * TURN * N_Y, bytes_accessed=4 * 2**20, transcendentals=0
        ),
    )(core, own, other)


def apply_kernel(core_ref, x_ref, mine_ref, other_ref, out_ref, wide, acc, direct, turned):
    for ref, half in ((mine_ref, core_ref[0]), (other_ref, 1 - core_ref[0])):
        top = pl.multiple_of(half * SIDE, SIDE)

        def block(m):
            return pl.ds(pl.multiple_of(top + m * SIDE, SIDE), SIDE)

        for y in range(N_Y):
            for z in range(N_Z):
                at = pl.ds(pl.multiple_of(top + z * SLAB, SLAB), SLAB)
                for m in range(8):
                    value = ref[z, y, m * SLAB : (m + 1) * SLAB]
                    direct[y, at, block(m)] = value
                    if m:
                        turned[y, at, block(m - 1)] = value
                first = top + z * EXTRA + y // 4 * (SIDE // 2)
                at = pl.ds(pl.multiple_of(first, EXTRA), EXTRA)
                value = ref[z, y, 8 * SLAB : PIECE]
                direct[y % 4, at, block(8)] = value
                turned[y % 4, at, block(7)] = value
    zero = jnp.zeros((SIDE, SIDE), BF)
    for i in range(N_Y):
        last = 9 if i < 4 else 8
        direct[i, 0:SIDE, last * SIDE : (last + 1) * SIDE] = zero
        direct[i, SIDE : 2 * SIDE, 0:SIDE] = zero
        turned[i, 0:SIDE, (last - 1) * SIDE : last * SIDE] = zero
        turned[i, SIDE : 2 * SIDE, 0:SIDE] = zero

    def times_gram(value):
        wide[:, 0:MOE_FF] = value
        wide[:, MOE_FF:WIDE] = value[:, 0:PAIR]
        acc[...] = jnp.zeros_like(acc)

        def step(width, i, carry):
            start = pl.multiple_of(i * 2 * SIDE, 2 * SIDE)
            acc[:, pl.ds(start, width)] += lax.dot_general(
                wide[:, pl.ds(start, 2 * SIDE)], direct[i, :, 0:width],
                (((1,), (0,)), ((), ())), preferred_element_type=F32,
            )
            acc[:, pl.ds(start, 2 * SIDE)] += lax.dot_general(
                wide[:, pl.ds(pl.multiple_of(start + SIDE, SIDE), width - SIDE)],
                turned[i, :, 0 : width - SIDE],
                (((1,), (1,)), ((), ())), preferred_element_type=F32,
            )
            return carry

        lax.fori_loop(0, 4, functools.partial(step, PAIR), 0)
        lax.fori_loop(4, N_Y, functools.partial(step, TURN), 0)
        return jnp.concatenate(
            [acc[:, 0:PAIR] + acc[:, MOE_FF:WIDE], acc[:, PAIR:MOE_FF]], axis=1
        )

    x = x_ref[...]
    first = times_gram(x).astype(BF)
    second = times_gram(first)
    fresh = SCALE * (3.4445 * x.astype(F32) - 4.775 * first.astype(F32) + 2.0315 * second)
    fresh = fresh.astype(BF)
    for q in range(4):
        out_ref[q] = fresh[:, q * 512 : (q + 1) * 512]


def apply_gram(core, x, mine, other):
    rows = x.shape[0]
    vmem = pl.BlockSpec(memory_space=pltpu.VMEM)
    return pl.pallas_call(
        apply_kernel,
        out_shape=jax.ShapeDtypeStruct((4, rows, 512), BF),
        in_specs=[pl.BlockSpec(memory_space=pltpu.SMEM)] + [vmem] * 3,
        out_specs=vmem,
        scratch_shapes=[
            pltpu.VMEM((rows, WIDE), BF),
            pltpu.VMEM((rows, WIDE), F32),
            pltpu.VMEM((N_Y, 2 * SIDE, PAIR), BF),
            pltpu.VMEM((N_Y, 2 * SIDE, TURN), BF),
        ],
        compiler_params=pltpu.CompilerParams(vmem_limit_bytes=40 * 2**20),
        cost_estimate=pl.CostEstimate(
            flops=4 * rows * MOE_FF * MOE_FF, bytes_accessed=5 * 2**20, transcendentals=0
        ),
    )(core, x, mine, other)


def exchange(value):
    groups = [[4 * p + q for q in range(4)] for p in range(N_Y // 2)]
    return lax.all_to_all(value, ("y", "c"), 0, 1, axis_index_groups=groups, tiled=True)


def shards(iterate):
    core = lax.axis_index("c").astype(jnp.int32)[None]
    own = lax.all_to_all(iterate, ("x", "zl"), split_axis=0, concat_axis=1, tiled=True)[0]
    strips = make_strips(core, own, swap_cores(own))
    count = N_Y * N_Z
    strips = strips.reshape(count, PIECE, SIDE)
    parts = lax.all_to_all(strips, ("zh", "y"), 0, 0, tiled=True)
    piece = parts.astype(F32).sum(0).astype(BF)
    copies = jnp.broadcast_to(piece[None], (count, PIECE, SIDE))
    mine = lax.all_to_all(copies, ("zh", "y"), 0, 0, tiled=True)
    mine = mine.reshape(N_Z, N_Y, PIECE, SIDE)
    fresh = apply_gram(core, own, mine, swap_cores(mine))
    return exchange(fresh)[:, None]


def solution(mesh):
    names = ("x", "zl", "zh", "y", "c")
    split = Mesh(mesh.devices.reshape(8, 2, N_Z, N_Y, 2), names)
    return jax.shard_map(
        shards,
        mesh=split,
        in_specs=(P(None, names, None),),
        out_specs=P(names[:2], names[2:], None, None),
        check_vma=False,
    )
```

```python
import functools
import math

import jax
import jax.numpy as jnp
from jax import lax
from jax.experimental import pallas as pl
from jax.experimental.pallas import tpu as pltpu
from jax.sharding import Mesh
from jax.sharding import PartitionSpec as P

D = 7168
MOE_FF = 2048
N_Y = 8
N_Z = 4
SIDE = 128
SLAB = SIDE // N_Z
STRIP = 8 * SIDE
PAIR = 10 * SIDE
TURN = 9 * SIDE
EXTRA = SIDE // 2 // N_Z
PIECE = 8 * SLAB + EXTRA
WIDE = MOE_FF + PAIR
SCALE = 0.2 * math.sqrt(max(D, MOE_FF))
BF = jnp.bfloat16
F32 = jnp.float32


def swap_cores(value):
    return lax.ppermute(value, "c", [(0, 1), (1, 0)])


def send_y(value, shift):
    return lax.ppermute(value, ("yh", "yl"), [(y, (y + shift) % N_Y) for y in range(N_Y)])


def strips_kernel(first_ref, *refs):
    out_ref, wide = refs[-2:]
    at = 0
    for ref in refs[:-2]:
        rows = ref.shape[0]
        wide[at : at + rows, 0:MOE_FF] = ref[...]
        wide[at : at + rows, MOE_FF : MOE_FF + 8 * SIDE] = ref[:, 0 : 8 * SIDE]
        at += rows

    def times(left, right, width):
        return lax.dot_general(
            wide[:, pl.ds(pl.multiple_of(left, SIDE), SIDE)],
            wide[:, pl.ds(pl.multiple_of(right, SIDE), width)],
            (((0,), (0,)), ((), ())), preferred_element_type=F32,
        )

    def strip(y, carry):
        start = (4 * y + first_ref[0]) * SIDE
        value = times(start, start, STRIP).astype(BF)
        low = (4 * lax.rem(y, 2) + first_ref[0]) * SIDE
        extra = times(low, low + 8 * SIDE, SIDE)
        extra = jnp.where(y < 2, extra[: SIDE // 2], extra[SIDE // 2 :]).astype(BF)
        for z in range(N_Z):
            for m in range(8):
                out_ref[z, y, m * SLAB : (m + 1) * SLAB] = value[
                    z * SLAB : (z + 1) * SLAB, m * SIDE : (m + 1) * SIDE
                ]
            out_ref[z, y, 8 * SLAB : PIECE] = extra[z * EXTRA : (z + 1) * EXTRA]
        return carry

    lax.fori_loop(0, N_Y // 2, strip, 0)


def make_strips(first, pieces):
    vmem = pl.BlockSpec(memory_space=pltpu.VMEM)
    rows = sum(piece.shape[0] for piece in pieces)
    return pl.pallas_call(
        strips_kernel,
        out_shape=jax.ShapeDtypeStruct((N_Z, N_Y // 2, PIECE, SIDE), BF),
        in_specs=[pl.BlockSpec(memory_space=pltpu.SMEM)] + [vmem] * len(pieces),
        out_specs=vmem,
        scratch_shapes=[pltpu.VMEM((rows, MOE_FF + 8 * SIDE), BF)],
        compiler_params=pltpu.CompilerParams(vmem_limit_bytes=32 * 2**20),
        cost_estimate=pl.CostEstimate(
            flops=rows * SIDE * TURN * N_Y, bytes_accessed=4 * 2**20, transcendentals=0
        ),
    )(first, *pieces)


def apply_kernel(where_ref, x_ref, *refs):
    out_ref, wide, acc, direct, turned = refs[6:]
    core, parity = where_ref[0], where_ref[1]

    def place(ref, half, odd, first_z):
        top = pl.multiple_of(half * SIDE, SIDE)

        def block(m):
            return pl.ds(pl.multiple_of(top + m * SIDE, SIDE), SIDE)

        for h in range(N_Y // 2):
            pair = 2 * h + odd
            low = 2 * (h % 2) + odd
            for j in range(ref.shape[0]):
                z = first_z + j
                at = pl.ds(pl.multiple_of(top + z * SLAB, SLAB), SLAB)
                for m in range(8):
                    value = ref[j, h, m * SLAB : (m + 1) * SLAB]
                    direct[pair, at, block(m)] = value
                    if m:
                        turned[pair, at, block(m - 1)] = value
                first = top + z * EXTRA + h // 2 * (SIDE // 2)
                at = pl.ds(pl.multiple_of(first, EXTRA), EXTRA)
                value = ref[j, h, 8 * SLAB : PIECE]
                direct[low, at, block(8)] = value
                turned[low, at, block(7)] = value

    for side, half in ((0, core), (3, 1 - core)):
        place(refs[side], half, parity, 0)
        place(refs[side + 1], half, 1 - parity, 0)
        place(refs[side + 2], half, 1 - parity, N_Z // 2)
    zero = jnp.zeros((SIDE, SIDE), BF)
    for i in range(N_Y):
        last = 9 if i < 4 else 8
        direct[i, 0:SIDE, last * SIDE : (last + 1) * SIDE] = zero
        direct[i, SIDE : 2 * SIDE, 0:SIDE] = zero
        turned[i, 0:SIDE, (last - 1) * SIDE : last * SIDE] = zero
        turned[i, SIDE : 2 * SIDE, 0:SIDE] = zero

    def times_gram(value):
        wide[:, 0:MOE_FF] = value
        wide[:, MOE_FF:WIDE] = value[:, 0:PAIR]
        acc[...] = jnp.zeros_like(acc)

        def step(width, i, carry):
            start = pl.multiple_of(i * 2 * SIDE, 2 * SIDE)
            acc[:, pl.ds(start, width)] += lax.dot_general(
                wide[:, pl.ds(start, 2 * SIDE)], direct[i, :, 0:width],
                (((1,), (0,)), ((), ())), preferred_element_type=F32,
            )
            acc[:, pl.ds(start, 2 * SIDE)] += lax.dot_general(
                wide[:, pl.ds(pl.multiple_of(start + SIDE, SIDE), width - SIDE)],
                turned[i, :, 0 : width - SIDE],
                (((1,), (1,)), ((), ())), preferred_element_type=F32,
            )
            return carry

        lax.fori_loop(0, 4, functools.partial(step, PAIR), 0)
        lax.fori_loop(4, N_Y, functools.partial(step, TURN), 0)
        return jnp.concatenate(
            [acc[:, 0:PAIR] + acc[:, MOE_FF:WIDE], acc[:, PAIR:MOE_FF]], axis=1
        )

    x = x_ref[...]
    first = times_gram(x).astype(BF)
    second = times_gram(first)
    fresh = SCALE * (3.4445 * x.astype(F32) - 4.775 * first.astype(F32) + 2.0315 * second)
    fresh = fresh.astype(BF)
    for q in range(4):
        out_ref[q] = fresh[:, q * 512 : (q + 1) * 512]


def apply_gram(where, x, pieces):
    rows = x.shape[0]
    vmem = pl.BlockSpec(memory_space=pltpu.VMEM)
    return pl.pallas_call(
        apply_kernel,
        out_shape=jax.ShapeDtypeStruct((4, rows, 512), BF),
        in_specs=[pl.BlockSpec(memory_space=pltpu.SMEM)] + [vmem] * 7,
        out_specs=vmem,
        scratch_shapes=[
            pltpu.VMEM((rows, WIDE), BF),
            pltpu.VMEM((rows, WIDE), F32),
            pltpu.VMEM((N_Y, 2 * SIDE, PAIR), BF),
            pltpu.VMEM((N_Y, 2 * SIDE, TURN), BF),
        ],
        compiler_params=pltpu.CompilerParams(vmem_limit_bytes=40 * 2**20),
        cost_estimate=pl.CostEstimate(
            flops=4 * rows * MOE_FF * MOE_FF, bytes_accessed=5 * 2**20, transcendentals=0
        ),
    )(where, x, *pieces)


def shards(iterate):
    core = lax.axis_index("c").astype(jnp.int32)
    parity = lax.axis_index("yl").astype(jnp.int32)
    own = lax.all_to_all(iterate, ("x", "zl"), split_axis=0, concat_axis=1, tiled=True)[0]
    half = own.shape[0] // 2
    near = jnp.concatenate([send_y(own[:half], 1), send_y(own[half:], -1)], 0)
    strips = make_strips((2 * parity + core)[None], [own, swap_cores(own), near, swap_cores(near)])
    count = N_Z * N_Y // 2
    strips = strips.reshape(count, PIECE, SIDE)
    parts = lax.all_to_all(strips, ("zh", "yh"), 0, 0, tiled=True)
    piece = parts.astype(F32).sum(0).astype(BF)
    copies = jnp.broadcast_to(piece[None], (count, PIECE, SIDE))
    same = lax.all_to_all(copies, ("zh", "yh"), 0, 0, tiled=True)
    same = same.reshape(N_Z, N_Y // 2, PIECE, SIDE)
    mine = [same, send_y(same[: N_Z // 2], 1), send_y(same[N_Z // 2 :], -1)]
    other = [swap_cores(value) for value in mine]
    fresh = apply_gram(jnp.stack([core, parity]), own, mine + other)
    out = lax.all_to_all(fresh, ("yl", "c"), 0, 1, tiled=True)
    return out[:, None]


def solution(mesh):
    names = ("x", "zl", "zh", "yh", "yl", "c")
    split = Mesh(mesh.devices.reshape(8, 2, N_Z, N_Y // 2, 2, 2), names)
    return jax.shard_map(
        shards,
        mesh=split,
        in_specs=(P(None, names, None),),
        out_specs=P(names[:2], names[2:], None, None),
        check_vma=False,
    )
```
